32 devices in a mesh: dp: 4 (over y, x), ep: 8 (over z, core).
Axes of the slice: x: 2, y: 2, z: 4, core: 2. Of those that a mesh axis runs over, the one named last changes fastest.
Arguments:
- tokens: bfloat16 [4, 256, 2048], P('dp', 'ep'), may hold values from -12 to 12
- cotangent: bfloat16 [4, 256, 2048], P('dp', 'ep'), may hold values from -6 to 6
- assign: int32 [4, 256, 8], P('dp', 'ep'), may hold values from 0 to 7, as said below
- w_router: bfloat16 [2048, 8], replicated, may hold values from -0.125 to 0.125
- w_gate: bfloat16 [8, 2048, 768], P('ep'), may hold values from -0.125 to 0.125
- w_up: bfloat16 [8, 2048, 768], P('ep'), may hold values from -0.125 to 0.125
- w_down: bfloat16 [8, 2048, 768], P('ep'), may hold values from -0.21875 to 0.21875
Outputs:
- grad_tokens: bfloat16 [4, 256, 2048], P('dp', 'ep')
- grad_router: float32 [2048, 8], replicated
- grad_gate: bfloat16 [8, 2048, 768], P('ep', 'dp')
- grad_up: bfloat16 [8, 2048, 768], P('ep', 'dp')
- grad_down: bfloat16 [8, 2048, 768], P('ep', 'dp')
The draws below stay inside these ranges and needn't reach their ends.
Inputs may be any that keep to these rules, and one draw needn't show every extreme that they name: `assign`: each token names 8 different experts; the routes of the 32 tokens of one device name one expert at most 32 times, and in every draw one expert is named exactly 32 times by the routes of every device.
All inputs are finite; a program needn't handle non-finite values.
Results may differ from the reference program's by a relative error of at most 0.015.
Values may be sent and summed in bfloat16 or wider, within the bound.
No kernel may reach another device: no remote copies, remote signals or barrier semaphores. Data moves between devices by JAX's collectives and lax.ppermute only.
A program may use at most 128 MiB of HBM per device.

```python
import jax
import jax.numpy as jnp
from jax import lax

D = 2048
FF = 768
TOP = 8
ITERS = 3
TOK_DEV = 32
EXPERTS = 8
REP_TOK = 256
SLOT = 32
N_DP = 4
N_EP = 8


def route_block(block_key, hot_expert):
    first_key, second_key, third_key, fourth_key = jax.random.split(block_key, 4)
    others_count = EXPERTS - 1
    other_order = jax.random.permutation(first_key, others_count).astype(jnp.int32)
    others = other_order + (other_order >= hot_expert).astype(jnp.int32)
    routes_total = TOK_DEV * TOP
    remaining = routes_total - SLOT
    base_count = remaining // others_count
    extra_count = remaining % others_count
    counts = base_count + (jnp.arange(others_count, dtype=jnp.int32) < extra_count).astype(jnp.int32)
    move_limit = max(0, min(base_count, SLOT - base_count - 1))
    pair_count = others_count // 2
    move_sizes = jax.random.randint(second_key, (pair_count,), 0, move_limit + 1).astype(jnp.int32)
    count_shift = jnp.zeros((others_count,), jnp.int32)
    count_shift = count_shift.at[0:2 * pair_count:2].add(-move_sizes).at[1:2 * pair_count:2].add(move_sizes)
    counts = counts + count_shift
    experts_all = jnp.concatenate([jnp.full((1,), hot_expert, jnp.int32), others])
    counts_all = jnp.concatenate([jnp.full((1,), SLOT, jnp.int32), counts])
    shuffle = jax.random.permutation(third_key, EXPERTS)
    experts_all = experts_all[shuffle]
    counts_all = counts_all[shuffle]
    run_bounds = jnp.cumsum(counts_all)
    position = jnp.arange(routes_total, dtype=jnp.int32)
    run_index = jnp.sum((run_bounds[None, :] <= position[:, None]).astype(jnp.int32), axis=1)
    sequence = experts_all[run_index]
    route_table = sequence.reshape(TOP, TOK_DEV).T
    return route_table[jax.random.permutation(fourth_key, TOK_DEV)]


def draw_assign(key, part):
    hot_expert = jax.random.randint(jax.random.fold_in(key, 11), (), 0, EXPERTS).astype(jnp.int32)
    block_keys = jax.random.split(jax.random.fold_in(key, 12), N_DP * (REP_TOK // TOK_DEV))
    blocks = jax.vmap(lambda block_key: route_block(block_key, hot_expert))(block_keys)
    return blocks.reshape(N_DP, REP_TOK, TOP).astype(jnp.int32)


def draw_tokens(key, part):
    noise_key = jax.random.fold_in(key, 21)
    drift_key = jax.random.fold_in(key, 22)
    noise_field = jax.random.normal(noise_key, (N_DP, REP_TOK, D), jnp.float32)
    drift_field = jax.random.normal(drift_key, (N_DP, 1, D), jnp.float32)
    ramp_profile = (jnp.arange(REP_TOK, dtype=jnp.float32) / REP_TOK)[None, :, None]
    return jnp.clip(noise_field + 1.5 * ramp_profile * drift_field, -12.0, 12.0).astype(jnp.bfloat16)


def level_of(stream_key, shape, cuts, least, largest):
    gain, own = 1.0, jax.random.fold_in(stream_key, 6)
    for dim, blocks in cuts:
        draws = jnp.exp(jax.random.uniform(jax.random.fold_in(own, dim), (blocks,), jnp.float32, least / len(cuts), largest / len(cuts)))
        gain = gain * jnp.repeat(draws, shape[dim] // blocks).reshape([-1 if axis == dim else 1 for axis in range(len(shape))])
    return gain


def gaussian(key, extent, deviation, bound, shards=(), held_as=jnp.bfloat16):
    factor_of = level_of(key, extent, shards, -0.22, 0.18) if shards else 1.0
    values = jax.random.normal(key, extent, jnp.float32) * deviation * factor_of
    return jnp.minimum(jnp.maximum(values, -bound), bound).astype(held_as)


def setup_inputs(seed: int = 0) -> dict:
    arg_keys = jax.random.split(jax.random.key(seed), 8)
    tokens = draw_tokens(jax.random.fold_in(arg_keys[7], 71), 0)
    cotangent = gaussian(arg_keys[1], (N_DP, REP_TOK, D), 1.0, 6.0, ((0, 4), (1, 8)))
    assign = draw_assign(jax.random.fold_in(arg_keys[7], 71), 0)
    w_router = gaussian(arg_keys[3], (D, EXPERTS), D ** -0.5, 0.125)
    w_gate = gaussian(arg_keys[4], (EXPERTS, D, FF), D ** -0.5, 0.125, ((0, 8),))
    w_up = gaussian(arg_keys[5], (EXPERTS, D, FF), D ** -0.5, 0.125, ((0, 8),))
    w_down = gaussian(arg_keys[6], (EXPERTS, D, FF), FF ** -0.5, 0.21875, ((0, 8),))
    return dict(tokens=tokens, cotangent=cotangent, assign=assign, w_router=w_router, w_gate=w_gate, w_up=w_up, w_down=w_down)


cos_scale = 48.0
eps_norm = 1e-06
contract_first = (((0,), (0,)), ((), ()))
contract_last = (((1,), (1,)), ((), ()))

def logit_map(flat_tokens, router):
    inner_products = jnp.dot(flat_tokens, router, precision=lax.Precision.HIGHEST)
    token_norm = jnp.sqrt(lax.optimization_barrier(jnp.sum(flat_tokens * flat_tokens, axis=1)) + eps_norm)
    column_norm = jnp.sqrt(lax.optimization_barrier(jnp.sum(router * router, axis=0)) + eps_norm)
    return cos_scale * inner_products / (token_norm[:, None] * column_norm[None, :])

def expert_backward(expert_rows, expert_cotangent, rows_gate, gate_matrix, up_matrix, down_matrix):
    gate_linear = jnp.dot(expert_rows, gate_matrix, preferred_element_type=jnp.float32)
    up_linear = jnp.dot(expert_rows, up_matrix, preferred_element_type=jnp.float32)
    sigmoid_gate = jax.nn.sigmoid(gate_linear)
    activation = gate_linear * sigmoid_gate
    product = activation * up_linear
    hidden = product.astype(jnp.bfloat16)
    weighted = (rows_gate[:, None] * product).astype(jnp.bfloat16)
    raw_back = jnp.dot(expert_cotangent, down_matrix, preferred_element_type=jnp.float32)
    gate_grad = lax.optimization_barrier(jnp.sum(raw_back * hidden.astype(jnp.float32), axis=1)).astype(jnp.bfloat16)
    scaled_back = rows_gate[:, None] * raw_back
    up_delta = (scaled_back * activation).astype(jnp.bfloat16)
    gate_delta = (scaled_back * up_linear * sigmoid_gate * (1.0 + gate_linear * (1.0 - sigmoid_gate))).astype(jnp.bfloat16)
    route_back = (lax.dot_general(gate_delta, gate_matrix, contract_last, preferred_element_type=jnp.float32) + lax.dot_general(up_delta, up_matrix, contract_last, preferred_element_type=jnp.float32)).astype(jnp.bfloat16)
    return (gate_grad, route_back, gate_delta, up_delta, weighted)

def reference(tokens, cotangent, assign, w_router, w_gate, w_up, w_down):
    replica_count, token_count, model_width = tokens.shape
    experts = w_router.shape[1]
    per_token = assign.shape[2]
    flat_tokens = tokens.reshape(-1, model_width).astype(jnp.float32)
    logits_flat, logit_vjp = jax.vjp(logit_map, flat_tokens, w_router.astype(jnp.float32))
    logits = logits_flat.reshape(replica_count, token_count, experts)
    kernel_start = jnp.exp(logits)
    kernel = kernel_start
    saved_steps = []
    for sweep_index in range(ITERS):
        column = lax.optimization_barrier(jnp.sum(kernel, axis=1, keepdims=True))
        scaled = kernel / column
        row_total = lax.optimization_barrier(jnp.sum(scaled, axis=2, keepdims=True))
        kernel = scaled / row_total
        saved_steps.append((column, scaled, row_total, kernel))
    expert_ids = jnp.arange(experts, dtype=jnp.int32)
    onehot = (assign[..., None] == expert_ids).astype(jnp.float32)
    picked = lax.optimization_barrier(jnp.sum(onehot * kernel[:, :, None, :], axis=3))
    picked_sum = lax.optimization_barrier(jnp.sum(picked, axis=2, keepdims=True))
    gates = picked / picked_sum
    gate_half = gates.astype(jnp.bfloat16)
    routes_total = replica_count * token_count * per_token
    flat_assign = assign.reshape(-1).astype(jnp.int32)
    route_order = jnp.argsort(flat_assign, stable=True).astype(jnp.int32)
    counts = lax.optimization_barrier(jnp.sum((flat_assign[:, None] == expert_ids).astype(jnp.int32), axis=0))
    starts = (jnp.cumsum(counts) - counts).astype(jnp.int32)
    capacity = N_DP * N_EP * SLOT
    padded_order = jnp.concatenate([route_order, jnp.zeros((capacity,), jnp.int32)])
    token_rows = tokens.reshape(-1, model_width)
    cotangent_rows = cotangent.reshape(-1, model_width)
    gate_flat = gate_half.reshape(-1).astype(jnp.float32)

    def per_expert(totals, expert):
        back_total, gate_total = totals
        route_index = lax.dynamic_slice(padded_order, (starts[expert],), (capacity,)).astype(jnp.int32)
        valid_rows = jnp.arange(capacity, dtype=jnp.int32) < counts[expert]
        token_index = (route_index // per_token).astype(jnp.int32)
        zero_half = jnp.zeros((), jnp.bfloat16)
        expert_rows = jnp.where(valid_rows[:, None], token_rows[token_index], zero_half)
        expert_cotangent = jnp.where(valid_rows[:, None], cotangent_rows[token_index], zero_half)
        rows_gate = jnp.where(valid_rows, gate_flat[route_index], 0.0)
        gate_grad, route_back, gate_delta, up_delta, weighted = expert_backward(expert_rows, expert_cotangent, rows_gate, w_gate[expert], w_up[expert], w_down[expert])
        grad_g = lax.dot_general(expert_rows, gate_delta, contract_first, preferred_element_type=jnp.float32).astype(jnp.bfloat16)
        grad_u = lax.dot_general(expert_rows, up_delta, contract_first, preferred_element_type=jnp.float32).astype(jnp.bfloat16)
        grad_d = lax.dot_general(expert_cotangent, weighted, contract_first, preferred_element_type=jnp.float32).astype(jnp.bfloat16)
        back_total = back_total.at[token_index].add(jnp.where(valid_rows[:, None], route_back.astype(jnp.float32), 0.0))
        gate_total = gate_total.at[route_index].add(jnp.where(valid_rows, gate_grad.astype(jnp.float32), 0.0))
        return ((back_total, gate_total), (grad_g, grad_u, grad_d))
    initial = (jnp.zeros((replica_count * token_count, model_width), jnp.float32), jnp.zeros((routes_total,), jnp.float32))
    (expert_back, gate_total), (grad_gate, grad_up, grad_down) = lax.scan(per_expert, initial, expert_ids)
    route_grad = gate_total.reshape(replica_count, token_count, per_token)
    picked_grad = (route_grad - lax.optimization_barrier(jnp.sum(route_grad * gates, axis=2, keepdims=True))) / picked_sum
    kernel_grad = lax.optimization_barrier(jnp.sum(onehot * picked_grad[..., None], axis=2))
    for sweep_index in reversed(range(ITERS)):
        column, scaled, row_total, kernel_step = saved_steps[sweep_index]
        scaled_grad = (kernel_grad - lax.optimization_barrier(jnp.sum(kernel_grad * kernel_step, axis=2, keepdims=True))) / row_total
        kernel_grad = (scaled_grad - lax.optimization_barrier(jnp.sum(scaled_grad * scaled, axis=1, keepdims=True))) / column
    logit_grad = kernel_grad * kernel_start
    router_back, grad_router = logit_vjp(logit_grad.reshape(-1, experts))
    grad_tokens = (expert_back + router_back).astype(jnp.bfloat16).reshape(tokens.shape)
    return (grad_tokens, grad_router, grad_gate, grad_up, grad_down)
```

```python
import functools

import jax
import jax.numpy as jnp
from jax import lax
from jax.experimental import pallas as pl
from jax.experimental.pallas import tpu as pltpu
from jax.sharding import PartitionSpec as P

ITERS = 3


cos_scale = 48.0
eps_norm = 1e-06
contract_first = (((0,), (0,)), ((), ()))
contract_last = (((1,), (1,)), ((), ()))


def logit_map(flat_tokens, router):
    inner_products = jnp.dot(flat_tokens, router, precision=lax.Precision.HIGHEST)
    token_norm = jnp.sqrt(jnp.sum(flat_tokens * flat_tokens, axis=1) + eps_norm)
    column_norm = jnp.sqrt(jnp.sum(router * router, axis=0) + eps_norm)
    return cos_scale * inner_products / (token_norm[:, None] * column_norm[None, :])


def expert_backward(expert_rows, expert_cotangent, rows_gate, gate_matrix, up_matrix, down_matrix):
    gate_linear = jnp.dot(expert_rows, gate_matrix, preferred_element_type=jnp.float32)
    up_linear = jnp.dot(expert_rows, up_matrix, preferred_element_type=jnp.float32)
    sigmoid_gate = jax.nn.sigmoid(gate_linear)
    activation = gate_linear * sigmoid_gate
    product = activation * up_linear
    hidden = product.astype(jnp.bfloat16)
    weighted = (rows_gate[:, None] * product).astype(jnp.bfloat16)
    raw_back = jnp.dot(expert_cotangent, down_matrix, preferred_element_type=jnp.float32)
    gate_grad = jnp.sum(raw_back * hidden.astype(jnp.float32), axis=1).astype(jnp.bfloat16)
    scaled_back = rows_gate[:, None] * raw_back
    up_delta = (scaled_back * activation).astype(jnp.bfloat16)
    gate_delta = (
        scaled_back * up_linear * sigmoid_gate * (1.0 + gate_linear * (1.0 - sigmoid_gate))
    ).astype(jnp.bfloat16)
    route_back = (
        lax.dot_general(gate_delta, gate_matrix, contract_last, preferred_element_type=jnp.float32)
        + lax.dot_general(up_delta, up_matrix, contract_last, preferred_element_type=jnp.float32)
    ).astype(jnp.bfloat16)
    return (gate_grad, route_back, gate_delta, up_delta, weighted)


def column_sums(values):
    return lax.psum(jnp.sum(values, axis=0), "ep")


def back_partials(kernel_grad, known_moments, saved_steps):
    partial_list = []
    for sweep_index in reversed(range(len(saved_steps))):
        column, scaled, row_total, kernel_step = saved_steps[sweep_index]
        scaled_grad = (
            kernel_grad - jnp.sum(kernel_grad * kernel_step, axis=1, keepdims=True)
        ) / row_total
        partial_list.append(jnp.sum(scaled_grad * scaled, axis=0))
        kernel_grad = (scaled_grad - known_moments[sweep_index][None, :]) / column[None, :]
    partials = jnp.stack(partial_list[::-1])
    return (partials, kernel_grad)


contract_last_dims = (((1,), (1,)), ((), ()))
ANY = pl.ANY


def column_norms(router_t):
    router = router_t.astype(jnp.float32)
    return jnp.sqrt(jnp.sum(router * router, axis=1, keepdims=True) + eps_norm)


def token_norms(token_ref, rows, width):
    total = jnp.zeros((rows.size, 128), jnp.float32)
    for start in range(0, width, 128):
        part = token_ref[rows, start : start + 128].astype(jnp.float32)
        total = total + part * part
    return jnp.sqrt(jnp.sum(total.T, axis=0, keepdims=True) + eps_norm)


def logits_of(router_t, token_ref, rows, width):
    inner = lax.dot_general(
        router_t, token_ref[rows, :width], contract_last_dims, preferred_element_type=jnp.float32
    )
    token_norm = token_norms(token_ref, rows, width)
    return cos_scale * inner / (token_norm * column_norms(router_t)), token_norm


def balance(kernel):
    saved = []
    for _ in range(ITERS):
        column = jnp.sum(kernel, axis=1, keepdims=True)
        scaled = kernel / column
        row_total = jnp.sum(scaled, axis=0, keepdims=True)
        kernel = scaled / row_total
        saved.append((column, scaled, row_total, kernel))
    return kernel, saved


def own_gate_column(kernel, expert):
    gates = kernel / jnp.sum(kernel, axis=0, keepdims=True)
    pick = lax.broadcasted_iota(jnp.int32, gates.shape, 0) == expert
    row = jnp.sum(jnp.where(pick, gates, 0.0), axis=0, keepdims=True)
    row = row.astype(jnp.bfloat16).astype(jnp.float32)
    return jnp.broadcast_to(row, (128, row.shape[1])).T


def expert_tile(tokens, cotangent, gate_column, wg, wu, wd):
    gate_linear = jnp.dot(tokens, wg, preferred_element_type=jnp.float32)
    up_linear = jnp.dot(tokens, wu, preferred_element_type=jnp.float32)
    raw_back = jnp.dot(cotangent, wd, preferred_element_type=jnp.float32)
    sigmoid_gate = jax.nn.sigmoid(gate_linear)
    activation = gate_linear * sigmoid_gate
    product = activation * up_linear
    weighted = (gate_column * product).astype(jnp.bfloat16)
    scaled_back = gate_column * raw_back
    up_delta = (scaled_back * activation).astype(jnp.bfloat16)
    gate_delta = (
        scaled_back * up_linear * sigmoid_gate * (1.0 + gate_linear * (1.0 - sigmoid_gate))
    ).astype(jnp.bfloat16)
    return raw_back, product, gate_delta, up_delta, weighted


def load_pieces(pieces, buffer, sems):
    row = 0
    copies = []
    for index, piece in enumerate(pieces):
        rows = piece.shape[0]
        copies.append(pltpu.make_async_copy(piece, buffer.at[pl.ds(row, rows)], sems.at[index]))
        row += rows
    for copy in copies:
        copy.start()
    for copy in copies:
        copy.wait()


def own_kernel(n_pieces, where_ref, *refs):
    pieces = refs[:n_pieces]
    (router_ref, wg_ref, wu_ref, wd_ref, gd_ref, ud_ref, wt_ref, back_ref, gg_ref, logit_ref, norm_ref,
     buffer, gate_ref, back_acc, gg_acc, sems) = refs[n_pieces:]
    tile = pl.program_id(0)
    count, width = buffer.shape[0], buffer.shape[1] // 2
    lanes = gate_ref.shape[1]

    @pl.when(tile == 0)
    def _():
        load_pieces(pieces, buffer, sems)
        logits, token_norm = logits_of(router_ref[...], buffer, pl.ds(0, count), width)
        kernel, _ = balance(jnp.exp(logits))
        gate_ref[...] = own_gate_column(kernel, where_ref[1])
        logit_ref[...] = logits
        norm_ref[...] = jnp.broadcast_to(token_norm, norm_ref.shape)
        back_acc[...] = jnp.zeros_like(back_acc)
        gg_acc[...] = jnp.zeros_like(gg_acc)

    gate_column = gate_ref[:, :1]
    wg, wu = wg_ref[0], wu_ref[0]
    raw_back, product, gate_delta, up_delta, weighted = expert_tile(
        buffer[:, :width], buffer[:, width:], gate_column, wg, wu, wd_ref[0]
    )
    gd_ref[...] = gate_delta
    ud_ref[...] = up_delta
    wt_ref[...] = weighted
    part = raw_back * product.astype(jnp.bfloat16).astype(jnp.float32)
    total = gg_acc[...]
    for start in range(0, part.shape[1], lanes):
        total = total + part[:, start : start + lanes]
    gg_acc[...] = total
    back_acc[...] += lax.dot_general(
        gate_delta, wg, contract_last_dims, preferred_element_type=jnp.float32
    ) + lax.dot_general(up_delta, wu, contract_last_dims, preferred_element_type=jnp.float32)

    @pl.when(tile == pl.num_programs(0) - 1)
    def _():
        back_ref[...] = back_acc[...].astype(back_ref.dtype)
        row = jnp.sum(gg_acc[...].T, axis=0, keepdims=True)
        gg_ref[...] = jnp.broadcast_to(row, gg_ref.shape).astype(gg_ref.dtype)


def others_kernel(n_own, n_other, rep_tokens, where_ref, *refs):
    own = refs[:n_own]
    other = refs[n_own : n_own + n_other]
    (router_ref, gd_ref, ud_ref, wt_ref, wg_ref, wu_ref, wd_ref, dg_ref, du_ref, dd_ref,
     own_tok, own_cot, buffer, gate_ref, tok_t, cot_t, sems, own_sems) = refs[n_own + n_other :]
    tile = pl.program_id(0)
    count, width = buffer.shape[0], buffer.shape[1] // 2
    part = tok_t.shape[0]

    @pl.when(tile == 0)
    def _():
        start = pl.multiple_of(where_ref[0] * part, part)
        copies = []
        row = 0
        for index, piece in enumerate(own):
            rows = piece.shape[0]
            copies.append(pltpu.make_async_copy(
                piece.at[:, pl.ds(start, part)], own_tok.at[pl.ds(row, rows)], own_sems.at[0, index]))
            copies.append(pltpu.make_async_copy(
                piece.at[:, pl.ds(width + start, part)], own_cot.at[pl.ds(row, rows)], own_sems.at[1, index]))
            row += rows
        for copy in copies:
            copy.start()
        load_pieces(other, buffer, sems)
        for copy in copies:
            copy.wait()
        tok_t[:, :rep_tokens] = own_tok[...].T
        cot_t[:, :rep_tokens] = own_cot[...].T
        for first in range(0, count, rep_tokens):
            rows = pl.ds(first, rep_tokens)
            logits, _ = logits_of(router_ref[...], buffer, rows, width)
            kernel, _ = balance(jnp.exp(logits))
            gate_ref[rows, :] = own_gate_column(kernel, where_ref[1])
            columns = pl.ds(rep_tokens + first, rep_tokens)
            tok_t[:, columns] = buffer[rows, pl.ds(start, part)].T
            cot_t[:, columns] = buffer[rows, pl.ds(width + start, part)].T

    gate_column = gate_ref[:, :1]
    _, _, gate_delta, up_delta, weighted = expert_tile(
        buffer[:, :width], buffer[:, width:], gate_column, wg_ref[0], wu_ref[0], wd_ref[0]
    )

    def total(first_ref, own_ref, others):
        return jnp.dot(
            first_ref[:, :rep_tokens], own_ref[...], preferred_element_type=jnp.float32
        ) + jnp.dot(first_ref[:, rep_tokens:], others, preferred_element_type=jnp.float32)

    dg_ref[0] = total(tok_t, gd_ref, gate_delta).astype(dg_ref.dtype)
    du_ref[0] = total(tok_t, ud_ref, up_delta).astype(du_ref.dtype)
    dd_ref[0] = total(cot_t, wt_ref, weighted).astype(dd_ref.dtype)


def split_three(value):
    high = value.astype(jnp.bfloat16)
    rest = value - high.astype(jnp.float32)
    middle = rest.astype(jnp.bfloat16)
    low = (rest - middle.astype(jnp.float32)).astype(jnp.bfloat16)
    return high, middle, low


def router_kernel(n_pieces, order, where_ref, *refs):
    pieces = refs[:n_pieces]
    gg = refs[n_pieces : n_pieces + len(order)]
    (router_ref, logit_ref, norm_ref, part_ref, back_ref, buffer, sems) = refs[n_pieces + len(order) :]
    experts, count = logit_ref.shape
    rows = pieces[0].shape[0]
    width = buffer.shape[1]
    copies = []
    for index, piece in enumerate(pieces):
        copies.append(pltpu.make_async_copy(
            piece.at[:, pl.ds(0, width)], buffer.at[pl.ds(index * rows, rows)], sems.at[index]))
    for copy in copies:
        copy.start()
    logits = logit_ref[...]
    token_norm = norm_ref[:1, :]
    router_t = router_ref[...]
    column_norm = column_norms(router_t)
    kernel_start = jnp.exp(logits)
    kernel, saved = balance(kernel_start)
    picked_sum = jnp.sum(kernel, axis=0, keepdims=True)
    gates = kernel / picked_sum
    sublane = lax.broadcasted_iota(jnp.int32, (experts, count), 0)
    route_grad = jnp.zeros((experts, count), jnp.float32)
    for ref, (shift, swap) in zip(gg, order):
        pairs = experts // 2
        owner = 2 * lax.rem(where_ref[1] // 2 - shift + pairs, pairs) + (
            where_ref[1] % 2 if swap == 0 else 1 - where_ref[1] % 2
        )
        row = ref[:1, :].astype(jnp.float32)
        route_grad = jnp.where(sublane == owner, row, route_grad)
    picked_grad = (route_grad - jnp.sum(route_grad * gates, axis=0, keepdims=True)) / picked_sum
    kernel_grad = picked_grad
    for column, scaled, row_total, kernel_step in reversed(saved):
        scaled_grad = (
            kernel_grad - jnp.sum(kernel_grad * kernel_step, axis=0, keepdims=True)
        ) / row_total
        kernel_grad = (
            scaled_grad - jnp.sum(scaled_grad * scaled, axis=1, keepdims=True)
        ) / column
    logit_grad = kernel_grad * kernel_start
    inner_grad = cos_scale * logit_grad / (token_norm * column_norm)
    products = logit_grad * logits
    router_scale = jnp.sum(products, axis=1, keepdims=True) / (column_norm * column_norm)
    token_scale = jnp.sum(products, axis=0, keepdims=True) / (token_norm * token_norm)
    for copy in copies:
        copy.wait()
    pieces3 = jnp.concatenate([p.astype(jnp.float32) for p in split_three(inner_grad)], axis=0)
    wide = jnp.dot(pieces3.astype(jnp.bfloat16), buffer[...], preferred_element_type=jnp.float32)
    router_f = router_t.astype(jnp.float32)
    part_ref[...] = (
        wide[:experts] + wide[experts : 2 * experts] + wide[2 * experts :]
    ) - router_f * router_scale
    lanes = 128
    stack = jnp.concatenate([pieces3, jnp.broadcast_to(token_scale, pieces3[:experts].shape)], axis=0)
    stack = jnp.concatenate(
        [stack[:, :lanes], jnp.zeros((lanes - stack.shape[0], lanes), jnp.float32)], axis=0
    ).T
    mine = stack[:rows, : 3 * experts].astype(jnp.bfloat16)
    router3 = jnp.concatenate([router_f, router_f, router_f], axis=0).astype(jnp.bfloat16)
    scale = stack[:rows, 3 * experts : 3 * experts + 1]
    back_ref[...] = jnp.dot(
        mine, router3, preferred_element_type=jnp.float32
    ) - buffer[:rows].astype(jnp.float32) * scale


def dense_device(tokens, cotangent, w_router, w_gate, w_up, w_down):
    n_dp, n_ep = lax.axis_size("dp"), lax.axis_size("ep")
    pairs = n_ep // 2
    rows, width = tokens.shape[1:]
    experts = w_router.shape[1]
    hidden = w_gate.shape[2]
    rep_tokens = rows * n_ep
    part = width // n_dp
    tile = 256 if hidden % 256 == 0 else hidden
    tiles = hidden // tile

    def core(value):
        return lax.ppermute(value, "ep", [(i, i ^ 1) for i in range(n_ep)])

    def along(value, shift):
        return lax.ppermute(value, "ep", [(i, (i + 2 * shift) % n_ep) for i in range(n_ep)])

    def replica(value, step):
        power = n_dp & (n_dp - 1) == 0
        return lax.ppermute(
            value, "dp", [(i, i ^ step if power else (i + step) % n_dp) for i in range(n_dp)]
        )

    where = jnp.stack([lax.axis_index("dp"), lax.axis_index("ep")]).astype(jnp.int32)
    router_t = w_router.T
    block = jnp.concatenate([tokens[0], cotangent[0]], axis=1)
    line = [block] + [along(block, shift) for shift in range(1, pairs)]
    partner = [core(value) for value in line]
    own = line + partner
    other = []
    for step in range(1, n_dp):
        mine = [replica(value, step) for value in line]
        other += mine + [core(value) for value in mine]

    any_spec = pl.BlockSpec(memory_space=ANY)
    whole = pl.BlockSpec(memory_space=pltpu.VMEM)
    weight_spec = pl.BlockSpec((1, width, tile), lambda j, w: (0, 0, j))
    delta_spec = pl.BlockSpec((rep_tokens, tile), lambda j, w: (0, j))
    full = lambda shape: pl.BlockSpec(shape, lambda j, w: (0, 0))
    half = jnp.bfloat16
    sds = jax.ShapeDtypeStruct
    gate_delta, up_delta, weighted, back, gate_grad, logits, norms = pl.pallas_call(
        functools.partial(own_kernel, len(own)),
        out_shape=(
            sds((rep_tokens, hidden), half),
            sds((rep_tokens, hidden), half),
            sds((rep_tokens, hidden), half),
            sds((rep_tokens, width), half),
            sds((16, rep_tokens), half),
            sds((experts, rep_tokens), jnp.float32),
            sds((8, rep_tokens), jnp.float32),
        ),
        grid_spec=pltpu.PrefetchScalarGridSpec(
            num_scalar_prefetch=1,
            grid=(tiles,),
            in_specs=[any_spec] * len(own) + [full((experts, width))] + [weight_spec] * 3,
            out_specs=(
                delta_spec, delta_spec, delta_spec, full((rep_tokens, width)), full((16, rep_tokens)),
                full((experts, rep_tokens)), full((8, rep_tokens)),
            ),
            scratch_shapes=[
                pltpu.VMEM((rep_tokens, 2 * width), half),
                pltpu.VMEM((rep_tokens, 128), jnp.float32),
                pltpu.VMEM((rep_tokens, width), jnp.float32),
                pltpu.VMEM((rep_tokens, 128), jnp.float32),
                pltpu.SemaphoreType.DMA((len(own),)),
            ],
        ),
        name="own_replica",
    )(where, *own, router_t, w_gate, w_up, w_down)

    count = rep_tokens * (n_dp - 1)
    grads = pl.pallas_call(
        functools.partial(others_kernel, len(own), len(other), rep_tokens),
        out_shape=tuple(sds((1, part, hidden), half) for _ in range(3)),
        grid_spec=pltpu.PrefetchScalarGridSpec(
            num_scalar_prefetch=1,
            grid=(tiles,),
            in_specs=[any_spec] * (len(own) + len(other))
            + [full((experts, width))]
            + [delta_spec] * 3
            + [weight_spec] * 3,
            out_specs=tuple(pl.BlockSpec((1, part, tile), lambda j, w: (0, 0, j)) for _ in range(3)),
            scratch_shapes=[
                pltpu.VMEM((rep_tokens, part), half),
                pltpu.VMEM((rep_tokens, part), half),
                pltpu.VMEM((count, 2 * width), half),
                pltpu.VMEM((count, 128), jnp.float32),
                pltpu.VMEM((part, rep_tokens + count), half),
                pltpu.VMEM((part, rep_tokens + count), half),
                pltpu.SemaphoreType.DMA((len(other),)),
                pltpu.SemaphoreType.DMA((2, len(own))),
            ],
        ),
        name="other_replicas",
    )(where, *own, *other, router_t, gate_delta, up_delta, weighted, w_gate, w_up, w_down)

    def turn(value, shift, swap):
        pieces = value.reshape(value.shape[0], 2, pairs, rows)
        if swap:
            pieces = jnp.flip(pieces, axis=1)
        return jnp.roll(pieces, shift, axis=2).reshape(value.shape)

    both = [gate_grad, core(gate_grad)]
    chip = jnp.concatenate(both, axis=0)
    order, gate_grads = [], []
    for shift in range(pairs):
        moved = chip if shift == 0 else along(chip, shift)
        for swap in range(2):
            order.append((shift, swap))
            gate_grads.append(turn(moved[16 * swap : 16 * swap + 16], shift, swap))

    half_rows = rows * pairs
    summed = (
        back[:half_rows].astype(jnp.float32) + core(back[half_rows:]).astype(jnp.float32)
    )
    returned = [
        along(summed[rows * s : rows * (s + 1)].astype(half), pairs - s) for s in range(1, pairs)
    ]

    router_part, router_back = pl.pallas_call(
        functools.partial(router_kernel, len(own), tuple(order)),
        out_shape=(sds((experts, width), jnp.float32), sds((rows, width), jnp.float32)),
        grid_spec=pltpu.PrefetchScalarGridSpec(
            num_scalar_prefetch=1,
            grid=(),
            in_specs=[any_spec] * len(own) + [whole] * (len(order) + 3),
            out_specs=(whole, whole),
            scratch_shapes=[
                pltpu.VMEM((rep_tokens, width), half),
                pltpu.SemaphoreType.DMA((len(own),)),
            ],
        ),
        name="router_backward",
    )(where, *own, *gate_grads, router_t, logits, norms)
    grad_router = router_part
    for step in range(1, n_dp):
        grad_router = grad_router + replica(router_part, step)
    grad_tokens = summed[:rows] + router_back
    for value in returned:
        grad_tokens = grad_tokens + value.astype(jnp.float32)
    return (grad_tokens.astype(half)[None], grad_router.T) + grads


def per_device(tokens, cotangent, assign, w_router, w_gate, w_up, w_down):
    n_ep = lax.axis_size("ep")
    if assign.shape[2] == w_router.shape[1] == n_ep and n_ep % 2 == 0:
        return dense_device(tokens, cotangent, w_router, w_gate, w_up, w_down)
    local_tokens = tokens[0]
    local_cotangent = cotangent[0]
    route_ids = assign[0]
    token_count, per_token = route_ids.shape
    model_width = local_tokens.shape[1]
    experts = w_router.shape[1]
    slot_cap = min(token_count, 2 * token_count * per_token // experts)
    logits, logit_vjp = jax.vjp(
        logit_map, local_tokens.astype(jnp.float32), w_router.astype(jnp.float32)
    )
    kernel_start = jnp.exp(logits)
    kernel = kernel_start
    saved_steps = []
    for sweep_index in range(ITERS):
        column = column_sums(kernel)
        scaled = kernel / column[None, :]
        row_total = jnp.sum(scaled, axis=1, keepdims=True)
        kernel = scaled / row_total
        saved_steps.append((column, scaled, row_total, kernel))
    expert_ids = jnp.arange(experts, dtype=jnp.int32)
    onehot = (route_ids[:, :, None] == expert_ids).astype(jnp.float32)
    picked = jnp.sum(onehot * kernel[:, None, :], axis=2)
    picked_sum = jnp.sum(picked, axis=1, keepdims=True)
    gates = picked / picked_sum
    gate_half = gates.astype(jnp.bfloat16)
    flat_route = route_ids.reshape(-1)
    member = (flat_route[:, None] == expert_ids).astype(jnp.int32)
    earlier = jnp.cumsum(member, axis=0) - member
    slot_index = jnp.sum(earlier * member, axis=1)
    target = flat_route * slot_cap + slot_index
    route_slots = (
        jnp.arange(experts * slot_cap, dtype=jnp.int32)[:, None] == target[None, :]
    ).astype(jnp.bfloat16)
    token_slots = jnp.sum(route_slots.reshape(experts * slot_cap, token_count, per_token), axis=2)
    send_tokens = jnp.dot(token_slots, local_tokens, preferred_element_type=jnp.float32).astype(
        jnp.bfloat16
    )
    send_cotangent = jnp.dot(
        token_slots, local_cotangent, preferred_element_type=jnp.float32
    ).astype(jnp.bfloat16)
    send_gate = jnp.dot(
        route_slots, gate_half.reshape(-1), preferred_element_type=jnp.float32
    ).astype(jnp.bfloat16)
    recv_tokens, recv_cotangent, recv_gate = (
        lax.all_to_all(
            send_tokens.reshape(experts, slot_cap, model_width),
            "ep",
            split_axis=0,
            concat_axis=0,
            tiled=True,
        ),
        lax.all_to_all(
            send_cotangent.reshape(experts, slot_cap, model_width),
            "ep",
            split_axis=0,
            concat_axis=0,
            tiled=True,
        ),
        lax.all_to_all(
            send_gate.reshape(experts, slot_cap), "ep", split_axis=0, concat_axis=0, tiled=True
        ),
    )
    expert_rows = recv_tokens.reshape(-1, model_width)
    expert_cotangent = recv_cotangent.reshape(-1, model_width)
    rows_gate = recv_gate.reshape(-1).astype(jnp.float32)
    gate_grad, route_back, gate_delta, up_delta, weighted = expert_backward(
        expert_rows, expert_cotangent, rows_gate, w_gate[0], w_up[0], w_down[0]
    )
    back_rows, back_gate = (
        lax.all_to_all(
            route_back.reshape(experts, slot_cap, model_width),
            "ep",
            split_axis=0,
            concat_axis=0,
            tiled=True,
        ),
        lax.all_to_all(
            gate_grad.reshape(experts, slot_cap), "ep", split_axis=0, concat_axis=0, tiled=True
        ),
    )
    expert_back = lax.dot_general(
        token_slots,
        back_rows.reshape(-1, model_width),
        contract_first,
        preferred_element_type=jnp.float32,
    )
    route_grad = lax.dot_general(
        route_slots, back_gate.reshape(-1), contract_first, preferred_element_type=jnp.float32
    ).reshape(token_count, per_token)
    hidden_units = gate_delta.shape[1]
    summed = lax.psum_scatter(
        jnp.concatenate(
            [
                lax.dot_general(
                    expert_rows, gate_delta, contract_first, preferred_element_type=jnp.float32
                ),
                lax.dot_general(
                    expert_rows, up_delta, contract_first, preferred_element_type=jnp.float32
                ),
                lax.dot_general(
                    expert_cotangent, weighted, contract_first, preferred_element_type=jnp.float32
                ),
            ],
            axis=1,
        ).astype(jnp.bfloat16),
        "dp",
        scatter_dimension=0,
        tiled=True,
    ).astype(jnp.float32)
    grad_gate = summed[:, :hidden_units]
    grad_up = summed[:, hidden_units : 2 * hidden_units]
    grad_down = summed[:, 2 * hidden_units :]
    picked_grad = (route_grad - jnp.sum(route_grad * gates, axis=1, keepdims=True)) / picked_sum
    kernel_grad = jnp.sum(onehot * picked_grad[:, :, None], axis=1)
    zero_known = jnp.zeros((ITERS, experts), jnp.float32)
    base_part, unused_grad = back_partials(kernel_grad, zero_known, saved_steps)
    basis_stack = jnp.eye(ITERS * experts, dtype=jnp.float32).reshape(
        ITERS * experts, ITERS, experts
    )
    zero_grad = jnp.zeros_like(kernel_grad)
    jacobian = jax.vmap(lambda direction: back_partials(zero_grad, direction, saved_steps)[0])(
        basis_stack
    )
    base_sum, jacobian_sum = lax.psum((base_part, jacobian), "ep")
    solved = jnp.zeros((ITERS * experts,), jnp.float32)
    for sweep_index in reversed(range(ITERS)):
        moment_value = base_sum[sweep_index] + jnp.sum(
            jacobian_sum[:, sweep_index, :] * solved[:, None], axis=0
        )
        solved = solved.at[sweep_index * experts : (sweep_index + 1) * experts].set(moment_value)
    unused_part, kernel_grad = back_partials(
        kernel_grad, solved.reshape(ITERS, experts), saved_steps
    )
    logit_grad = kernel_grad * kernel_start
    router_back, router_part = logit_vjp(logit_grad)
    grad_router = lax.psum(router_part, ("dp", "ep"))
    grad_tokens = (expert_back + router_back).astype(jnp.bfloat16)[None]
    return (
        grad_tokens,
        grad_router,
        grad_gate.astype(jnp.bfloat16)[None],
        grad_up.astype(jnp.bfloat16)[None],
        grad_down.astype(jnp.bfloat16)[None],
    )


def solution(mesh):
    return jax.shard_map(
        per_device,
        mesh=mesh,
        in_specs=(
            P("dp", "ep", None),
            P("dp", "ep", None),
            P("dp", "ep", None),
            P(),
            P("ep", None, None),
            P("ep", None, None),
            P("ep", None, None),
        ),
        out_specs=(
            P("dp", "ep", None),
            P(),
            P("ep", "dp", None),
            P("ep", "dp", None),
            P("ep", "dp", None),
        ),
        check_vma=False,
    )
```
